256 devices in a mesh: dp: 16 (over z, core), expert: 16 (over y, x).
Axes of the slice: x: 4, y: 4, z: 8, core: 2. Of those that a mesh axis runs over, the one named last changes fastest.
Arguments:
- tokens: bfloat16 [32768, 2048], P(('dp', 'expert')), may hold values from -6 to 6
- expert_ids: int32 [32768, 2], P(('dp', 'expert')), may hold values from 0 to 7, all different within a row; in each aligned block of 128 rows (0 to 127, 128 to 255, ...) at most 40 rows name the same one
- gate_values: bfloat16 [32768, 2], P(('dp', 'expert')), may hold values from 0.19921875 to 0.796875
- w_gate: bfloat16 [16, 2048, 896], P('expert', 'dp'), may hold values from -0.125 to 0.125
- w_up: bfloat16 [16, 2048, 896], P('expert', 'dp'), may hold values from -0.125 to 0.125
- w_down: bfloat16 [16, 896, 2048], P('expert', 'dp'), may hold values from -0.0625 to 0.0625
- cotangent: bfloat16 [32768, 2048], P(('dp', 'expert')), may hold values from -6 to 6
- momentum: bfloat16 [16, 896, 2048], P('expert', 'dp'), may hold values from -4 to 4
- worker_error: bfloat16 [16, 16, 896, 2048], P('dp', 'expert'), may hold values from -2 to 2
- server_error: float32 [16, 896, 2048], P('expert', 'dp'), may hold values from -2 to 2
Outputs:
- outputs: bfloat16 [32768, 2048], P(('dp', 'expert'))
- new_momentum: bfloat16 [16, 896, 2048], P('expert', 'dp')
- new_worker_error: bfloat16 [16, 16, 896, 2048], P('dp', 'expert')
- new_server_error: float32 [16, 896, 2048], P('expert', 'dp')
The draws below stay inside these ranges and needn't reach their ends.
Inputs may be any that keep to these rules, and one draw needn't show every extreme that they name: `expert_ids`: A token names 2 different experts. Among the 128 tokens of one device at most 40 name the same expert, and some device reaches 40.
All inputs are finite; a program needn't handle non-finite values. Where the reference program divides by a largest or mean magnitude, that divisor is 1e-20 or more.
Results may differ from the reference program's by a relative error of at most 0.009.
Values may be sent and summed in bfloat16 or wider, within the bound.
No kernel may reach another device: no remote copies, remote signals or barrier semaphores. Data moves between devices by JAX's collectives and lax.ppermute only.
A program may use at most 128 MiB of HBM per device.

```python
import math
import jax
import jax.numpy as jnp
import numpy as np
from jax import lax

D = 2048
E = 8
EW = 2
FF = 7168
TOP = 2
T_DEV = 128
CAP = 40
S = 8
HS = 896
NB = 16
TOKENS = 32768
N_DP = 16
N_EXPERT = 16


def block_scale(rng, shape, shards, smallest, largest):
    def one(dim, shards_of):
        draws = jax.random.uniform(jax.random.fold_in(jax.random.fold_in(rng, 6), dim), (shards_of,), jnp.float32, smallest / len(shards), largest / len(shards))
        return jnp.repeat(jnp.exp(draws), shape[dim] // shards_of).reshape((-1,) + (1,) * (len(shape) - dim - 1))

    gain = one(*shards[0])
    for cut in shards[1:]:
        gain = gain * one(*cut)
    return gain


def routed_block(key, own, number, rows, count, top, limit, skew):
    ranking = jax.random.permutation(key, count)
    packed, usual = portions_of(count, rows * top, limit, skew, True), portions_of(count, rows * top, limit, skew, False)
    places = jnp.arange(count)

    def named(lengths, offset_by):
        used = int((lengths > 0).sum())
        fixed = max(1, used // 4)
        passed = fixed + (places - fixed + offset_by * (used - fixed)) % max(1, count - fixed)
        return jnp.zeros((count,), jnp.int32).at[ranking[jnp.where(places < fixed, places, passed)]].set(jnp.asarray(lengths, jnp.int32))

    lengths = jnp.where(number % 4 == 0, named(packed, number // 4), named(usual, number - number // 4 - 1))
    mixed = jax.random.permutation(jax.random.fold_in(own, 3), count)
    source_of, sink = mixed[0:count // 2 * 2:2], mixed[1:count // 2 * 2:2]
    slack = jnp.minimum(lengths[source_of] - 1, limit - lengths[sink]) // 2
    slack = jnp.where((source_of == ranking[0]) | (sink == ranking[0]) | (lengths[sink] == 0), 0, jnp.maximum(slack, 0))
    passed = jax.random.randint(jax.random.fold_in(own, 4), (count // 2,), 0, 1 << 20) % (slack + 1)
    lengths = lengths.at[source_of].add(-passed).at[sink].add(passed)
    items = jnp.searchsorted(jnp.cumsum(lengths), jnp.arange(rows * top), side="right").astype(jnp.int32)
    table = items.reshape(top, rows).T
    table = table[jax.random.permutation(jax.random.fold_in(own, 1), rows)]
    offset_by = jax.random.randint(jax.random.fold_in(own, 2), (rows, 1), 0, top)
    return jnp.take_along_axis(table, (jnp.arange(top)[None, :] + offset_by) % top, axis=1)


def portions_of(number_of, total, limit, slope, full):
    weights = [(1 << 20) // math.isqrt(grade ** slope) + 1 for grade in range(1, number_of + 1)]
    largest = limit if full else min(limit, max(-(-total // number_of), total * weights[0] // sum(weights)))
    least = 1 if total - largest >= number_of - 1 else 0
    counts, rest = [largest] + [least] * (number_of - 1), total - largest - least * (number_of - 1)
    while rest > 0:
        free = [i for i in range(1, number_of) if counts[i] < largest] or [i for i in range(1, number_of) if counts[i] < limit]
        whole, remaining = sum([weights[i] for i in free]), rest
        for i in free:
            addition = min(limit - counts[i], max(1, remaining * weights[i] // whole), rest)
            counts[i] = counts[i] + addition
            rest = rest - addition
    return np.array(counts)


def scatter_about(rng, dims, scale, reach, shards=(), held_as=jnp.bfloat16):
    drawn = scale * jax.random.normal(rng, dims, jnp.float32)
    if shards:
        drawn = drawn * block_scale(rng, dims, shards, -0.22, 0.18)
    return jnp.clip(drawn, -reach, reach).astype(held_as)


def setup_inputs(seed: int = 0) -> dict:
    streams_of = jax.random.split(jax.random.key(seed), 11)
    tokens = scatter_about(streams_of[0], (TOKENS, D), 1.0, 6.0, ((0, 256),))
    expert_ids_keys = jax.random.split(jax.random.fold_in(streams_of[1], 1), TOKENS // T_DEV)
    expert_ids_turns = jax.random.permutation(jax.random.fold_in(streams_of[1], 3), TOKENS // T_DEV)
    expert_ids = jax.vmap(lambda own, number: routed_block(jax.random.fold_in(streams_of[1], 2), own, number, T_DEV, E, TOP, CAP, 2))(expert_ids_keys, expert_ids_turns).reshape((TOKENS, TOP))
    gate_values = jnp.clip(0.19921875 + 0.59765625 * jax.random.uniform(streams_of[2], (TOKENS, TOP), jnp.float32) ** block_scale(streams_of[2], (TOKENS, TOP), ((0, 256),), -0.2, 0.2), 0.19921875, 0.796875).astype(jnp.bfloat16)
    w_gate = scatter_about(streams_of[3], (NB, D, HS), D ** -0.5, 0.125, ((0, 16), (1, 16)))
    w_up = scatter_about(streams_of[4], (NB, D, HS), D ** -0.5, 0.125, ((0, 16), (1, 16)))
    w_down = scatter_about(streams_of[5], (NB, HS, D), FF ** -0.5, 0.0625, ((0, 16), (1, 16)))
    cotangent = scatter_about(streams_of[6], (TOKENS, D), 1.0, 6.0, ((0, 256),))
    momentum = scatter_about(streams_of[7], (NB, HS, D), 0.5, 4.0, ((0, 16), (1, 16)))
    worker_error = scatter_about(streams_of[8], (N_DP, NB, HS, D), 0.2, 2.0, ((0, 16), (1, 16)))
    server_error = scatter_about(streams_of[9], (NB, HS, D), 0.2, 2.0, ((0, 16), (1, 16)), jnp.float32)
    return {"tokens": tokens, "expert_ids": expert_ids, "gate_values": gate_values, "w_gate": w_gate, "w_up": w_up, "w_down": w_down, "cotangent": cotangent, "momentum": momentum, "worker_error": worker_error, "server_error": server_error}


def squash(values):
    scale = jnp.mean(jnp.abs(values), axis=-1, keepdims=True) + 1e-6
    return (scale * jnp.tanh(values / scale)).astype(jnp.bfloat16)


def slot_position(ids_dev):
    flat = ids_dev.reshape(-1)
    onehot = (flat[:, None] == jnp.arange(E, dtype=jnp.int32)[None, :]).astype(jnp.int32)
    ranks = jnp.sum((jnp.cumsum(onehot, axis=0) - onehot) * onehot, axis=1)
    return jnp.where(flat < EW, flat * CAP + ranks, EW * CAP).astype(jnp.int32)


def pick_rows(source, index):
    return source[index]


def add_rows(total, index, values):
    return total.at[index].add(values)


def reference(tokens, expert_ids, gate_values, w_gate, w_up, w_down, cotangent, momentum, worker_error, server_error):
    devices = N_DP * N_EXPERT
    position = jax.vmap(slot_position)(expert_ids.reshape(devices, T_DEV, TOP))
    owner = jnp.broadcast_to(jnp.repeat(jnp.arange(T_DEV, dtype=jnp.int32), TOP)[None, :], position.shape)
    device_rows = jnp.broadcast_to(jnp.arange(devices, dtype=jnp.int32)[:, None], position.shape)
    table = jnp.full((devices, EW * CAP + 1), T_DEV, jnp.int32).at[device_rows, position].set(owner)
    gate_table = jnp.zeros((devices, EW * CAP + 1), jnp.float32).at[device_rows, position].set(
        gate_values.reshape(devices, T_DEV * TOP).astype(jnp.float32))
    table = table[:, :EW * CAP].reshape(devices, EW, CAP)
    gate_table = gate_table[:, :EW * CAP].reshape(devices, EW, CAP)
    padding = jnp.zeros((devices, 1, D), jnp.bfloat16)
    token_rows = jnp.concatenate([tokens.reshape(devices, T_DEV, D), padding], axis=1)
    cot_rows = jnp.concatenate([cotangent.reshape(devices, T_DEV, D), padding], axis=1)

    def one_block(total, block):
        expert = block // S
        index = lax.dynamic_index_in_dim(table, expert, 1, False)
        gates = lax.dynamic_index_in_dim(gate_table, expert, 1, False).reshape(-1)
        rows = jax.vmap(pick_rows)(token_rows, index).reshape(devices * CAP, D)
        gate_w = lax.dynamic_index_in_dim(w_gate, block, 0, False)
        up_w = lax.dynamic_index_in_dim(w_up, block, 0, False)
        down_w = lax.dynamic_index_in_dim(w_down, block, 0, False)
        gate_h = jnp.dot(rows, gate_w, preferred_element_type=jnp.float32)
        up_h = jnp.dot(rows, up_w, preferred_element_type=jnp.float32)
        hidden = (jax.nn.silu(gate_h) * up_h).astype(jnp.bfloat16)
        partial_value = jnp.dot(hidden, down_w, preferred_element_type=jnp.float32).astype(jnp.bfloat16)
        term = (gates[:, None] * partial_value.astype(jnp.float32)).reshape(devices, CAP, D)
        total = jax.vmap(add_rows)(total, index, term)
        weighted = (hidden.astype(jnp.float32) * gates[:, None]).astype(jnp.bfloat16)
        dy_rows = jax.vmap(pick_rows)(cot_rows, index).reshape(N_DP, N_EXPERT * CAP, D)
        grad = jnp.einsum("rnh,rnd->rhd", weighted.reshape(N_DP, N_EXPERT * CAP, HS).astype(jnp.float32),
                          dy_rows.astype(jnp.float32))
        previous = lax.dynamic_index_in_dim(momentum, block, 0, False).astype(jnp.float32)
        error = lax.dynamic_index_in_dim(worker_error, block, 1, False).astype(jnp.float32)
        corrected = 0.9 * previous[None] + 0.1 * grad + error
        sent = squash(corrected)
        new_error = (corrected - sent.astype(jnp.float32)).astype(jnp.bfloat16)
        average = jnp.sum(sent.astype(jnp.float32), axis=0) / N_DP
        server_in = average + lax.dynamic_index_in_dim(server_error, block, 0, False)
        new_mom = squash(server_in)
        new_server = server_in - new_mom.astype(jnp.float32)
        return total, (new_mom, new_error, new_server)

    start = jnp.zeros((devices, T_DEV + 1, D), jnp.float32)
    total, (moms, errors, servers) = lax.scan(one_block, start, jnp.arange(NB, dtype=jnp.int32))
    outputs = total[:, :T_DEV].reshape(devices * T_DEV, D).astype(jnp.bfloat16)
    return outputs, moms, jnp.transpose(errors, (1, 0, 2, 3)), servers
```

```python
import jax
import jax.numpy as jnp
import numpy as np
from jax import lax
from jax.sharding import Mesh
from jax.sharding import PartitionSpec as P

E = 8
EW = 2
TOP = 2
CAP = 40


def squash(values):
    scale = jnp.mean(jnp.abs(values), axis=-1, keepdims=True) + 1e-06
    return (scale * jnp.tanh(values / scale)).astype(jnp.bfloat16)


def swap_cores(value):
    return lax.ppermute(value, "core", [(0, 1), (1, 0)])


def gather_halves(piece):
    own = lax.all_gather(piece, "z", axis=0, tiled=False)
    return own, swap_cores(own)


def in_order(own, other):
    first = lax.axis_index("core") == 0
    pair = jnp.stack([jnp.where(first, own, other), jnp.where(first, other, own)], axis=1)
    return pair.reshape(-1, pair.shape[-1])


def per_device(
    tokens,
    expert_ids,
    gate_values,
    w_gate,
    w_up,
    w_down,
    cotangent,
    momentum,
    worker_error,
    server_error,
):
    n_expert = lax.axis_size("expert")
    n_z = lax.axis_size("z")
    n_replica = n_z * lax.axis_size("core")
    core = lax.axis_index("core")
    tok_count = tokens.shape[0]
    width = tokens.shape[1]
    hidden_units = w_gate.shape[2]
    slots = EW * CAP
    share = n_expert // EW
    flat = expert_ids.reshape(-1)
    onehot = (flat[:, None] == jnp.arange(E, dtype=jnp.int32)[None, :]).astype(jnp.int32)
    ranks = jnp.sum((jnp.cumsum(onehot, axis=0) - onehot) * onehot, axis=1)
    position = jnp.where(flat < EW, flat * CAP + ranks, -1)
    select = (position[None, :] == jnp.arange(slots, dtype=jnp.int32)[:, None]).reshape(
        slots, tok_count, TOP
    )
    dispatch = jnp.any(select, axis=2).astype(jnp.bfloat16)
    combine_w = jnp.sum(jnp.where(select, gate_values.astype(jnp.float32)[None], 0.0), axis=2)
    slot_gates = jnp.sum(combine_w, axis=1).astype(jnp.bfloat16).reshape(EW, CAP)
    peer_owner = np.arange(n_expert) // share
    mix = jnp.asarray((peer_owner[:, None] == np.arange(EW)[None, :]).astype(np.float32)).astype(
        jnp.bfloat16
    )

    def spread(buffer):
        return jnp.take(buffer, jnp.asarray(peer_owner, dtype=jnp.int32), axis=0)

    def slot_rows(source):
        return (
            jnp.dot(dispatch, source, preferred_element_type=jnp.float32)
            .astype(jnp.bfloat16)
            .reshape(EW, CAP, width)
        )

    by_core = tokens.reshape(tok_count, n_z, 2, -1)
    even = by_core[:, :, 0].reshape(tok_count, width // 2)
    odd = by_core[:, :, 1].reshape(tok_count, width // 2)
    own_first = jnp.concatenate(
        [jnp.where(core == 0, even, odd), jnp.where(core == 0, odd, even)], axis=1
    )
    send_rows = spread(slot_rows(own_first))
    send_gates = spread(slot_gates)
    got_rows, got_gates = (
        lax.all_to_all(send_rows, "expert", split_axis=0, concat_axis=0, tiled=True),
        lax.all_to_all(send_gates, "expert", split_axis=0, concat_axis=0, tiled=True),
    )
    rows = got_rows.reshape(n_expert * CAP, width)
    gate_own, gate_other = gather_halves(w_gate[0])
    up_own, up_other = gather_halves(w_up[0])

    def project(own, other):
        half = width // 2
        return jnp.dot(
            rows[:, :half], own.reshape(half, hidden_units), preferred_element_type=jnp.float32
        ) + jnp.dot(
            rows[:, half:], other.reshape(half, hidden_units), preferred_element_type=jnp.float32
        )

    gate_h = project(gate_own, gate_other)
    up_h = project(up_own, up_other)
    hidden = (jax.nn.silu(gate_h) * up_h).astype(jnp.bfloat16)
    down_full = in_order(*gather_halves(w_down[0]))
    mom_full = in_order(*gather_halves(momentum[0]))
    partial_value = jnp.dot(hidden, down_full, preferred_element_type=jnp.float32).astype(
        jnp.bfloat16
    )
    returned = lax.all_to_all(
        partial_value.reshape(n_expert, CAP, width),
        "expert",
        split_axis=0,
        concat_axis=0,
        tiled=True,
    )
    expert_sum = jnp.einsum("kcd,ke->ecd", returned, mix, preferred_element_type=jnp.float32)
    outputs = jnp.einsum(
        "pt,pd->td",
        combine_w,
        expert_sum.reshape(slots, width),
        precision=lax.Precision.HIGHEST,
        preferred_element_type=jnp.float32,
    ).astype(jnp.bfloat16)
    got_cot = lax.all_to_all(
        spread(slot_rows(cotangent)), "expert", split_axis=0, concat_axis=0, tiled=True
    )
    dy_rows = got_cot.reshape(n_expert * CAP, width)
    gate_rows = got_gates.reshape(n_expert * CAP).astype(jnp.float32)
    weighted = (hidden.astype(jnp.float32) * gate_rows[:, None]).astype(jnp.bfloat16)
    grad = jnp.einsum("rh,rd->hd", weighted, dy_rows, preferred_element_type=jnp.float32)
    corrected = (
        0.9 * mom_full.astype(jnp.float32) + 0.1 * grad + worker_error[0, 0].astype(jnp.float32)
    )
    sent = squash(corrected)
    new_worker = (corrected - sent.astype(jnp.float32)).astype(jnp.bfloat16)[None, None]
    pieces = sent.reshape(n_z, 2, hidden_units // n_replica, width)
    kept = jnp.where(core == 0, pieces[:, 0], pieces[:, 1])
    passed = jnp.where(core == 0, pieces[:, 1], pieces[:, 0])
    pair_sum = (kept.astype(jnp.float32) + swap_cores(passed).astype(jnp.float32)).astype(
        jnp.bfloat16
    )
    total = lax.psum_scatter(pair_sum, "z", scatter_dimension=0, tiled=False)
    average = total.astype(jnp.float32) / n_replica
    server_in = average + server_error[0]
    served = squash(server_in)
    new_server = (server_in - served.astype(jnp.float32))[None]
    return (outputs, served[None], new_worker, new_server)


def solution(mesh):
    shape = (mesh.shape["dp"] // 2, 2, mesh.shape["expert"])
    split = Mesh(mesh.devices.reshape(shape), ("z", "core", "expert"))
    return jax.shard_map(
        per_device,
        mesh=split,
        in_specs=(
            P(("z", "core", "expert"), None),
            P(("z", "core", "expert"), None),
            P(("z", "core", "expert"), None),
            P("expert", ("z", "core"), None),
            P("expert", ("z", "core"), None),
            P("expert", ("z", "core"), None),
            P(("z", "core", "expert"), None),
            P("expert", ("z", "core"), None),
            P(("z", "core"), "expert", None, None),
            P("expert", ("z", "core"), None),
        ),
        out_specs=(
            P(("z", "core", "expert"), None),
            P("expert", ("z", "core"), None),
            P(("z", "core"), "expert", None, None),
            P("expert", ("z", "core"), None),
        ),
        check_vma=False,
    )
```

```python
import jax
import jax.numpy as jnp
import numpy as np
from jax import lax
from jax.sharding import Mesh
from jax.sharding import PartitionSpec as P

E = 8
EW = 2
TOP = 2
CAP = 40


def squash(values):
    scale = jnp.mean(jnp.abs(values), axis=-1, keepdims=True) + 1e-06
    return (scale * jnp.tanh(values / scale)).astype(jnp.bfloat16)


def swap_cores(value):
    return lax.ppermute(value, "core", [(0, 1), (1, 0)])


def ring(value, n):
    up = [(i, (i + 1) % n) for i in range(n)]
    down = [(i, (i - 1) % n) for i in range(n)]
    below, above = [value], [value]
    for _ in range(n // 2 - 1):
        below.append(lax.ppermute(below[-1], "z", up))
        above.append(lax.ppermute(above[-1], "z", down))
    half = value.shape[1] // 2
    far = jnp.concatenate(
        [
            lax.ppermute(below[-1][:, :half], "z", up),
            lax.ppermute(above[-1][:, half:], "z", down),
        ],
        axis=1,
    )
    near = n // 4
    early = below[near:0:-1] + above[: near + 1]
    late = above[near + 1 :] + [far] + below[:near:-1]
    return jnp.stack(early, axis=1), jnp.stack(late, axis=1)


def per_device(
    tokens,
    expert_ids,
    gate_values,
    w_gate,
    w_up,
    w_down,
    cotangent,
    momentum,
    worker_error,
    server_error,
):
    n_expert = lax.axis_size("expert")
    n_z = lax.axis_size("z")
    n_replica = n_z * lax.axis_size("core")
    core = lax.axis_index("core")
    tok_count = tokens.shape[0]
    width = tokens.shape[1]
    hidden_units = w_gate.shape[2]
    slots = EW * CAP
    share = n_expert // EW
    flat = expert_ids.reshape(-1)
    onehot = (flat[:, None] == jnp.arange(E, dtype=jnp.int32)[None, :]).astype(jnp.int32)
    ranks = jnp.sum((jnp.cumsum(onehot, axis=0) - onehot) * onehot, axis=1)
    position = jnp.where(flat < EW, flat * CAP + ranks, -1)
    select = (position[None, :] == jnp.arange(slots, dtype=jnp.int32)[:, None]).reshape(
        slots, tok_count, TOP
    )
    dispatch = jnp.any(select, axis=2).astype(jnp.bfloat16)
    combine_w = jnp.sum(jnp.where(select, gate_values.astype(jnp.float32)[None], 0.0), axis=2)
    slot_gates = jnp.sum(combine_w, axis=1).astype(jnp.bfloat16).reshape(EW, CAP)
    peer_owner = np.arange(n_expert) // share
    mix = jnp.asarray((peer_owner[:, None] == np.arange(EW)[None, :]).astype(np.float32)).astype(
        jnp.bfloat16
    )

    def spread(buffer):
        return jnp.take(buffer, jnp.asarray(peer_owner, dtype=jnp.int32), axis=0)

    def slot_rows(source):
        return (
            jnp.dot(dispatch, source, preferred_element_type=jnp.float32)
            .astype(jnp.bfloat16)
            .reshape(EW, CAP, width)
        )

    zpos = lax.axis_index("z")
    by_core = tokens.reshape(tok_count, n_z, 2, -1)
    even = by_core[:, :, 0].reshape(tok_count, width // 2)
    odd = by_core[:, :, 1].reshape(tok_count, width // 2)
    first = (zpos - n_z // 4) % n_z
    shift = first * (width // 2 // n_z)

    def turned(half):
        return lax.dynamic_slice_in_dim(
            jnp.concatenate([half, half], axis=1), shift, width // 2, axis=1
        )

    own_first = jnp.concatenate(
        [turned(jnp.where(core == 0, even, odd)), turned(jnp.where(core == 0, odd, even))], axis=1
    )
    send_rows = spread(slot_rows(own_first))
    send_gates = spread(slot_gates)
    got_rows, got_gates = (
        lax.all_to_all(send_rows, "expert", split_axis=0, concat_axis=0, tiled=True),
        lax.all_to_all(send_gates, "expert", split_axis=0, concat_axis=0, tiled=True),
    )
    rows = got_rows.reshape(n_expert * CAP, width)
    near, far = ring(jnp.stack([w_gate[0], w_up[0]]), n_z)
    w_down, momentum, near, far = lax.optimization_barrier((w_down, momentum, near, far))
    parts = (near, far, swap_cores(near), swap_cores(far))
    gate_h = up_h = 0.0
    start = 0
    for part in parts:
        weight = part.reshape(2, -1, hidden_units)
        piece = rows[:, start : start + weight.shape[1]]
        start += weight.shape[1]
        gate_h = gate_h + jnp.dot(piece, weight[0], preferred_element_type=jnp.float32)
        up_h = up_h + jnp.dot(piece, weight[1], preferred_element_type=jnp.float32)
    near, far = ring(jnp.stack([w_down[0], momentum[0]]), n_z)
    both = jnp.concatenate([near, far, swap_cores(near), swap_cores(far)], axis=1)
    places = jnp.arange(n_z, dtype=jnp.int32)[:, None]
    places = (places - first) % n_z + n_z * (jnp.arange(2, dtype=jnp.int32)[None] != core)

    def in_order(pieces):
        return jnp.take(pieces, places.reshape(-1), axis=0).reshape(hidden_units, width)

    hidden = (jax.nn.silu(gate_h) * up_h).astype(jnp.bfloat16)
    down_full = in_order(both[0])
    mom_full = in_order(both[1])
    partial_value = jnp.dot(hidden, down_full, preferred_element_type=jnp.float32).astype(
        jnp.bfloat16
    )
    returned = lax.all_to_all(
        partial_value.reshape(n_expert, CAP, width),
        "expert",
        split_axis=0,
        concat_axis=0,
        tiled=True,
    )
    expert_sum = jnp.einsum("kcd,ke->ecd", returned, mix, preferred_element_type=jnp.float32)
    outputs = jnp.einsum(
        "pt,pd->td",
        combine_w,
        expert_sum.reshape(slots, width),
        precision=lax.Precision.HIGHEST,
        preferred_element_type=jnp.float32,
    ).astype(jnp.bfloat16)
    got_cot = lax.all_to_all(
        spread(slot_rows(cotangent)), "expert", split_axis=0, concat_axis=0, tiled=True
    )
    dy_rows = got_cot.reshape(n_expert * CAP, width)
    gate_rows = got_gates.reshape(n_expert * CAP).astype(jnp.float32)
    weighted = (hidden.astype(jnp.float32) * gate_rows[:, None]).astype(jnp.bfloat16)
    grad = jnp.einsum("rh,rd->hd", weighted, dy_rows, preferred_element_type=jnp.float32)
    corrected = (
        0.9 * mom_full.astype(jnp.float32) + 0.1 * grad + worker_error[0, 0].astype(jnp.float32)
    )
    sent = squash(corrected)
    new_worker = (corrected - sent.astype(jnp.float32)).astype(jnp.bfloat16)[None, None]
    pieces = sent.reshape(n_z, 2, hidden_units // n_replica, width)
    kept = jnp.where(core == 0, pieces[:, 0], pieces[:, 1])
    passed = jnp.where(core == 0, pieces[:, 1], pieces[:, 0])
    pair_sum = (kept.astype(jnp.float32) + swap_cores(passed).astype(jnp.float32)).astype(
        jnp.bfloat16
    )
    total = lax.psum_scatter(pair_sum, "z", scatter_dimension=0, tiled=False)
    average = total.astype(jnp.float32) / n_replica
    server_in = average + server_error[0]
    served = squash(server_in)
    new_server = (server_in - served.astype(jnp.float32))[None]
    return (outputs, served[None], new_worker, new_server)


def solution(mesh):
    shape = (mesh.shape["dp"] // 2, 2, mesh.shape["expert"])
    split = Mesh(mesh.devices.reshape(shape), ("z", "core", "expert"))
    return jax.shard_map(
        per_device,
        mesh=split,
        in_specs=(
            P(("z", "core", "expert"), None),
            P(("z", "core", "expert"), None),
            P(("z", "core", "expert"), None),
            P("expert", ("z", "core"), None),
            P("expert", ("z", "core"), None),
            P("expert", ("z", "core"), None),
            P(("z", "core", "expert"), None),
            P("expert", ("z", "core"), None),
            P(("z", "core"), "expert", None, None),
            P("expert", ("z", "core"), None),
        ),
        out_specs=(
            P(("z", "core", "expert"), None),
            P("expert", ("z", "core"), None),
            P(("z", "core"), "expert", None, None),
            P("expert", ("z", "core"), None),
        ),
        check_vma=False,
    )
```

```python
import jax
import jax.numpy as jnp
import numpy as np
from jax import lax
from jax.sharding import Mesh
from jax.sharding import PartitionSpec as P

E = 8
EW = 2
TOP = 2
CAP = 40


def squash(values):
    scale = jnp.mean(jnp.abs(values), axis=-1, keepdims=True) + 1e-06
    return (scale * jnp.tanh(values / scale)).astype(jnp.bfloat16)


def swap_cores(value):
    return lax.ppermute(value, "core", [(0, 1), (1, 0)])


def ring(value, n):
    up = [(i, (i + 1) % n) for i in range(n)]
    down = [(i, (i - 1) % n) for i in range(n)]
    below, above = [value], [value]
    for _ in range(n // 2 - 1):
        below.append(lax.ppermute(below[-1], "z", up))
        above.append(lax.ppermute(above[-1], "z", down))
    half = value.shape[1] // 2
    far = jnp.concatenate(
        [
            lax.ppermute(below[-1][:, :half], "z", up),
            lax.ppermute(above[-1][:, half:], "z", down),
        ],
        axis=1,
    )
    near = n // 4
    early = below[near:0:-1] + above[: near + 1]
    late = above[near + 1 :] + [far] + below[:near:-1]
    return jnp.stack(early, axis=1), jnp.stack(late, axis=1)


def per_device(
    tokens,
    expert_ids,
    gate_values,
    w_gate,
    w_up,
    w_down,
    cotangent,
    momentum,
    worker_error,
    server_error,
):
    n_expert = lax.axis_size("expert")
    n_z = lax.axis_size("z")
    n_replica = n_z * lax.axis_size("core")
    core = lax.axis_index("core")
    tok_count = tokens.shape[0]
    width = tokens.shape[1]
    hidden_units = w_gate.shape[2]
    slots = EW * CAP
    share = n_expert // EW
    flat = expert_ids.reshape(-1)
    onehot = (flat[:, None] == jnp.arange(E, dtype=jnp.int32)[None, :]).astype(jnp.int32)
    ranks = jnp.sum((jnp.cumsum(onehot, axis=0) - onehot) * onehot, axis=1)
    position = jnp.where(flat < EW, flat * CAP + ranks, -1)
    select = (position[None, :] == jnp.arange(slots, dtype=jnp.int32)[:, None]).reshape(
        slots, tok_count, TOP
    )
    dispatch = jnp.any(select, axis=2).astype(jnp.bfloat16)
    combine_w = jnp.sum(jnp.where(select, gate_values.astype(jnp.float32)[None], 0.0), axis=2)
    slot_gates = jnp.sum(combine_w, axis=1).astype(jnp.bfloat16).reshape(EW, CAP)
    peer_owner = np.arange(n_expert) // share
    mix = jnp.asarray((peer_owner[:, None] == np.arange(EW)[None, :]).astype(np.float32)).astype(
        jnp.bfloat16
    )

    def spread(buffer):
        return jnp.take(buffer, jnp.asarray(peer_owner, dtype=jnp.int32), axis=0)

    def slot_rows(source):
        return (
            jnp.dot(dispatch, source, preferred_element_type=jnp.float32)
            .astype(jnp.bfloat16)
            .reshape(EW, CAP, width)
        )

    zpos = lax.axis_index("z")
    first = (zpos - n_z // 4) % n_z
    send_rows = spread(slot_rows(tokens))
    send_gates = spread(slot_gates)
    got_rows, got_gates = (
        lax.all_to_all(send_rows, "expert", split_axis=0, concat_axis=0, tiled=True),
        lax.all_to_all(send_gates, "expert", split_axis=0, concat_axis=0, tiled=True),
    )
    rows = got_rows.reshape(n_expert * CAP, width)
    gate_full = lax.all_gather(w_gate, ("z", "core"), axis=1, tiled=True)
    up_full = lax.all_gather(w_up, ("z", "core"), axis=1, tiled=True)
    gate_h = jnp.dot(rows, gate_full[0], preferred_element_type=jnp.float32)
    up_h = jnp.dot(rows, up_full[0], preferred_element_type=jnp.float32)
    near, far = ring(jnp.stack([w_down[0], momentum[0]]), n_z)
    both = jnp.concatenate([near, far, swap_cores(near), swap_cores(far)], axis=1)
    places = jnp.arange(n_z, dtype=jnp.int32)[:, None]
    places = (places - first) % n_z + n_z * (jnp.arange(2, dtype=jnp.int32)[None] != core)

    def in_order(pieces):
        return jnp.take(pieces, places.reshape(-1), axis=0).reshape(hidden_units, width)

    hidden = (jax.nn.silu(gate_h) * up_h).astype(jnp.bfloat16)
    down_full = in_order(both[0])
    mom_full = in_order(both[1])
    partial_value = jnp.dot(hidden, down_full, preferred_element_type=jnp.float32).astype(
        jnp.bfloat16
    )
    returned = lax.all_to_all(
        partial_value.reshape(n_expert, CAP, width),
        "expert",
        split_axis=0,
        concat_axis=0,
        tiled=True,
    )
    expert_sum = jnp.einsum("kcd,ke->ecd", returned, mix, preferred_element_type=jnp.float32)
    outputs = jnp.einsum(
        "pt,pd->td",
        combine_w,
        expert_sum.reshape(slots, width),
        precision=lax.Precision.HIGHEST,
        preferred_element_type=jnp.float32,
    ).astype(jnp.bfloat16)
    got_cot = lax.all_to_all(
        spread(slot_rows(cotangent)), "expert", split_axis=0, concat_axis=0, tiled=True
    )
    dy_rows = got_cot.reshape(n_expert * CAP, width)
    gate_rows = got_gates.reshape(n_expert * CAP).astype(jnp.float32)
    weighted = (hidden.astype(jnp.float32) * gate_rows[:, None]).astype(jnp.bfloat16)
    grad = jnp.einsum("rh,rd->hd", weighted, dy_rows, preferred_element_type=jnp.float32)
    corrected = (
        0.9 * mom_full.astype(jnp.float32) + 0.1 * grad + worker_error[0, 0].astype(jnp.float32)
    )
    sent = squash(corrected)
    new_worker = (corrected - sent.astype(jnp.float32)).astype(jnp.bfloat16)[None, None]
    pieces = sent.reshape(n_z, 2, hidden_units // n_replica, width)
    kept = jnp.where(core == 0, pieces[:, 0], pieces[:, 1])
    passed = jnp.where(core == 0, pieces[:, 1], pieces[:, 0])
    pair_sum = (kept.astype(jnp.float32) + swap_cores(passed).astype(jnp.float32)).astype(
        jnp.bfloat16
    )
    total = lax.psum_scatter(pair_sum, "z", scatter_dimension=0, tiled=False)
    average = total.astype(jnp.float32) / n_replica
    server_in = average + server_error[0]
    served = squash(server_in)
    new_server = (server_in - served.astype(jnp.float32))[None]
    return (outputs, served[None], new_worker, new_server)


def solution(mesh):
    shape = (mesh.shape["dp"] // 2, 2, mesh.shape["expert"])
    split = Mesh(mesh.devices.reshape(shape), ("z", "core", "expert"))
    return jax.shard_map(
        per_device,
        mesh=split,
        in_specs=(
            P(("z", "core", "expert"), None),
            P(("z", "core", "expert"), None),
            P(("z", "core", "expert"), None),
            P("expert", ("z", "core"), None),
            P("expert", ("z", "core"), None),
            P("expert", ("z", "core"), None),
            P(("z", "core", "expert"), None),
            P("expert", ("z", "core"), None),
            P(("z", "core"), "expert", None, None),
            P("expert", ("z", "core"), None),
        ),
        out_specs=(
            P(("z", "core", "expert"), None),
            P("expert", ("z", "core"), None),
            P(("z", "core"), "expert", None, None),
            P("expert", ("z", "core"), None),
        ),
        check_vma=False,
    )
```
